32 devices in a mesh: groups: 2 (over y), ctx: 4 (over x, core), mp: 4 (over z).
Axes of the slice: x: 2, y: 2, z: 4, core: 2. Of those that a mesh axis runs over, the one named last changes fastest.
Arguments:
- tokens: bfloat16 [3072, 8192], P(('groups', 'ctx')), parts along dimension 0, may hold values from -6 to 6
- norm_gain: bfloat16 [8192], replicated, may hold values from 0.099609375 to 1.8984375
- w_query: bfloat16 [8192, 4096], P('ctx', 'mp'), may hold values from -0.44194174 to 0.44194174
- w_key: bfloat16 [8192, 1024], P('ctx', 'mp'), may hold values from -0.044194174 to 0.044194174
- value_weight: bfloat16 [8192, 1024], P('ctx', 'mp'), may hold values from -0.0625 to 0.0625
- slab_order: int32 [8], P('groups'), parts along dimension 0, may hold values from 0 to 3, each once
- segment_ids: int32 [3072], P('groups'), parts along dimension 0, may hold values from 0 to 3, as said below
Outputs:
- attended: bfloat16 [3072, 4096], P(('groups', 'ctx'), 'mp'), parts along dimension 0
The draws below stay inside these ranges and needn't reach their ends.
There are 2 independent parts, one for each index of `groups`. The reference program is written for one: setup_inputs(seed, part) draws one part's arguments, and reference() takes and returns one part's arrays. A program takes and returns all parts, laid end to end along the dimension named above; an argument that names none is the same for every part. Nothing has to cross between parts.
Inputs may be any that keep to these rules, and one draw needn't show every extreme that they name: `segment_ids`: never falling along positions; each of the 4 segments holds at least one position.
All inputs are finite; a program needn't handle non-finite values.
Results may differ from the reference program's by a relative error of at most 0.012.
Values may be sent and summed in bfloat16 or wider, within the bound.
A program may use at most 128 MiB of HBM per device.

```python
import math
import jax
import jax.numpy as jnp
from jax import lax

MODEL_WIDTH = 8192
QUERY_HEADS = 32
KEY_VALUE_HEADS = 8
HEAD_SIZE = 128
SLABS = 4
TOKENS = 1536


def attention_pair(key):
    base = jax.random.fold_in(key, 11)
    leading_key = jax.random.fold_in(base, 1)
    second_key = jax.random.fold_in(base, 2)
    key_matrix = jnp.clip(jax.random.normal(leading_key, (MODEL_WIDTH, KEY_VALUE_HEADS * HEAD_SIZE), jnp.float32), -4.0, 4.0) * MODEL_WIDTH ** (-0.5)
    noise = jnp.clip(jax.random.normal(second_key, (MODEL_WIDTH, QUERY_HEADS * HEAD_SIZE), jnp.float32), -4.0, 4.0) * (3.0 * MODEL_WIDTH ** (-0.5))
    query_weight = noise
    return (query_weight, key_matrix)


def draw_w_query(key, part):
    query_weight, key_matrix = attention_pair(key)
    return query_weight.astype(jnp.bfloat16)


def draw_w_key(key, part):
    query_weight, key_matrix = attention_pair(key)
    return key_matrix.astype(jnp.bfloat16)


def draw_segment_ids(key, part):
    cut_key = jax.random.fold_in(key, 5)
    cuts = jax.random.permutation(cut_key, jnp.arange(TOKENS - 1, dtype=jnp.int32))[:3] + 1
    places = jnp.arange(TOKENS, dtype=jnp.int32)
    return jnp.sum((places[:, None] >= cuts[None, :]).astype(jnp.int32), axis=1).astype(jnp.int32)


def block_levels(rng, dims, pieces, smallest, largest):
    loudness = 1.0
    for dim, parts in pieces:
        draws = jax.random.uniform(jax.random.fold_in(jax.random.fold_in(rng, 6), dim), (parts,), jnp.float32, smallest / len(pieces), largest / len(pieces))
        loudness = loudness * jnp.repeat(jnp.exp(draws), dims[dim] // parts).reshape((-1,) + (1,) * (len(dims) - 1 - dim))
    return loudness


def normal_values(own_key, dims, deviation, limit, pieces=(), held_as=jnp.bfloat16):
    loudness = block_levels(own_key, dims, pieces, -0.22, 0.18) if pieces else 1.0
    array = jax.random.normal(own_key, dims, jnp.float32) * deviation * loudness
    return jnp.minimum(jnp.maximum(array, -limit), limit).astype(held_as)


def setup_inputs(seed: int = 0, part: int = 0) -> dict:
    arg_keys = jax.random.split(jax.random.key(seed), 8)
    part_keys = jax.random.split(jax.random.fold_in(arg_keys[7], part), 8)
    return {
        "tokens": normal_values(part_keys[0], (TOKENS, MODEL_WIDTH), 1.0, 6.0, ((0, 4),)),
        "norm_gain": jnp.clip(1.0 + 0.18 * jax.random.normal(arg_keys[1], (MODEL_WIDTH,), jnp.float32), 0.099609375, 1.8984375).astype(jnp.bfloat16),
        "w_query": draw_w_query(jax.random.fold_in(arg_keys[7], 71), part),
        "w_key": draw_w_key(jax.random.fold_in(arg_keys[7], 71), part),
        "value_weight": normal_values(arg_keys[4], (MODEL_WIDTH, KEY_VALUE_HEADS * HEAD_SIZE), MODEL_WIDTH ** -0.5, 0.0625, ((0, 4), (1, 4))),
        "slab_order": jax.random.permutation(part_keys[5], SLABS).astype(jnp.int32),
        "segment_ids": draw_segment_ids(jax.random.fold_in(jax.random.fold_in(arg_keys[7], part), 71), part),
    }


def apply_rotary(values, positions, heads):
    width = values.shape[1] // heads
    half = width // 2
    freqs = jnp.exp(jnp.arange(half, dtype=jnp.float32) * (-2.0 * math.log(500000.0) / width))
    angles = positions.astype(jnp.float32)[:, None] * freqs[None, :]
    cosine = jnp.cos(angles)[:, None, :]
    sine = jnp.sin(angles)[:, None, :]
    shaped = values.reshape(values.shape[0], heads, width)
    first = shaped[..., :half]
    second = shaped[..., half:]
    turned = jnp.concatenate([first * cosine - second * sine, second * cosine + first * sine], axis=-1)
    return turned.reshape(values.shape)

def reference(tokens, norm_gain, w_query, w_key, value_weight, slab_order, segment_ids):
    seq_len = tokens.shape[0]
    slab_rows = seq_len // SLABS
    token_position = (slab_order[:, None] * slab_rows + jnp.arange(slab_rows, dtype=jnp.int32)[None, :]).reshape(-1).astype(jnp.int32)
    segment = jnp.take(segment_ids, token_position)
    floats = tokens.astype(jnp.float32)
    inverse = lax.rsqrt(lax.optimization_barrier(jnp.mean(floats * floats, axis=-1, keepdims=True)) + 1e-05)
    normed = (floats * inverse * norm_gain.astype(jnp.float32)[None, :]).astype(jnp.bfloat16)
    query = jnp.dot(normed, w_query, preferred_element_type=jnp.float32)
    key_projected = jnp.dot(normed, w_key, preferred_element_type=jnp.float32)
    value_proj = jnp.dot(normed, value_weight, preferred_element_type=jnp.float32)
    query_rot = apply_rotary(query, token_position, QUERY_HEADS).astype(jnp.bfloat16)
    key_rotary = apply_rotary(key_projected, token_position, KEY_VALUE_HEADS).astype(jnp.bfloat16)
    value_b = value_proj.astype(jnp.bfloat16)
    group_width = QUERY_HEADS // KEY_VALUE_HEADS
    allowed = (token_position[None, :] <= token_position[:, None]) & (segment[None, :] == segment[:, None])
    scale = HEAD_SIZE ** (-0.5)

    def one_head(head):
        kv_head = head // group_width
        query_head = lax.dynamic_slice_in_dim(query_rot, head * HEAD_SIZE, HEAD_SIZE, 1)
        key_head = lax.dynamic_slice_in_dim(key_rotary, kv_head * HEAD_SIZE, HEAD_SIZE, 1)
        value_head = lax.dynamic_slice_in_dim(value_b, kv_head * HEAD_SIZE, HEAD_SIZE, 1)
        scores = jnp.dot(query_head, key_head.T, preferred_element_type=jnp.float32) * scale
        scores = jnp.where(allowed, scores, -1e+30)
        row_peak = lax.optimization_barrier(jnp.max(scores, axis=-1, keepdims=True))
        exps = jnp.where(allowed, jnp.exp(scores - row_peak), 0.0)
        weights = exps.astype(jnp.bfloat16)
        mixed = jnp.dot(weights, value_head, preferred_element_type=jnp.float32)
        return (mixed / lax.optimization_barrier(jnp.sum(exps, axis=-1, keepdims=True))).astype(jnp.bfloat16)
    per_head = lax.map(one_head, jnp.arange(QUERY_HEADS, dtype=jnp.int32))
    return jnp.transpose(per_head, (1, 0, 2)).reshape(seq_len, QUERY_HEADS * HEAD_SIZE)
```

```python
import math

import jax
import jax.numpy as jnp
from jax import lax
from jax.experimental import pallas as pl
from jax.experimental.pallas import tpu as pltpu
from jax.sharding import PartitionSpec as P

HEAD_SIZE = 128


def apply_rotary(values, positions, heads):
    width = values.shape[1] // heads
    half = width // 2
    freqs = jnp.exp(jnp.arange(half, dtype=jnp.float32) * (-2.0 * math.log(500000.0) / width))
    angles = positions.astype(jnp.float32)[:, None] * freqs[None, :]
    cosine = jnp.cos(angles)[:, None, :]
    sine = jnp.sin(angles)[:, None, :]
    shaped = values.reshape(values.shape[0], heads, width)
    first = shaped[..., :half]
    second = shaped[..., half:]
    turned = jnp.concatenate(
        [first * cosine - second * sine, second * cosine + first * sine], axis=-1
    )
    return turned.reshape(values.shape)


def local_plain(tokens, norm_gain, w_query, w_key, value_weight, slab_order, segment_ids):
    tok_rows = tokens.shape[0]
    device_slab = lax.axis_index("ctx")
    position_all = (
        slab_order[:, None] * tok_rows + jnp.arange(tok_rows, dtype=jnp.int32)[None, :]
    ).reshape(-1)
    segment_all = jnp.take(segment_ids, position_all)
    my_position = lax.dynamic_slice_in_dim(position_all, device_slab * tok_rows, tok_rows)
    my_segment = lax.dynamic_slice_in_dim(segment_all, device_slab * tok_rows, tok_rows)
    floats = tokens.astype(jnp.float32)
    inverse = lax.rsqrt(jnp.mean(floats * floats, axis=-1, keepdims=True) + 1e-05)
    normed = (floats * inverse * norm_gain.astype(jnp.float32)[None, :]).astype(jnp.bfloat16)
    query_cols = w_query.shape[1]
    key_cols = w_key.shape[1]
    query = jnp.dot(
        normed,
        lax.all_gather(w_query, "ctx", axis=0, tiled=True),
        preferred_element_type=jnp.float32,
    )
    key_projected = jnp.dot(
        normed, lax.all_gather(w_key, "ctx", axis=0, tiled=True), preferred_element_type=jnp.float32
    )
    value_proj = jnp.dot(
        normed,
        lax.all_gather(value_weight, "ctx", axis=0, tiled=True),
        preferred_element_type=jnp.float32,
    )
    head_size = HEAD_SIZE
    heads_here = query_cols // head_size
    kv_here = key_cols // head_size
    group_width = heads_here // kv_here
    query_rot = (
        apply_rotary(query, my_position, heads_here)
        .astype(jnp.bfloat16)
        .reshape(tok_rows, kv_here, group_width, head_size)
    )
    key_rotary = apply_rotary(key_projected, my_position, kv_here).astype(jnp.bfloat16)
    value_b = value_proj.astype(jnp.bfloat16)
    scale = head_size ** (-0.5)
    start_state = (
        jnp.full((kv_here, group_width, tok_rows), -1e30, jnp.float32),
        jnp.zeros((kv_here, group_width, tok_rows), jnp.float32),
        jnp.zeros((kv_here, group_width, tok_rows, head_size), jnp.float32),
    )
    state = start_state
    key_piece = lax.all_gather(key_rotary, "ctx", axis=0, tiled=True)
    value_piece = lax.all_gather(value_b, "ctx", axis=0, tiled=True)
    piece_rows = key_piece.shape[0]
    block_rows = math.gcd(piece_rows, 1024)
    block_count = piece_rows // block_rows
    key_blocks = key_piece.reshape(block_count, block_rows, kv_here, head_size)
    value_blocks = value_piece.reshape(block_count, block_rows, kv_here, head_size)
    key_positions = position_all.reshape(block_count, block_rows)
    key_segments = segment_all.reshape(block_count, block_rows)

    def advance(inner, item):
        key_block, value_block, block_positions, block_segments = item
        allowed = (block_positions[None, :] <= my_position[:, None]) & (
            block_segments[None, :] == my_segment[:, None]
        )
        running_max, running_sum, running_acc = inner
        scores = (
            jnp.einsum("tkgd,nkd->kgtn", query_rot, key_block, preferred_element_type=jnp.float32)
            * scale
        )
        scores = jnp.where(allowed[None, None], scores, -1e30)
        new_max = jnp.maximum(running_max, jnp.max(scores, axis=-1))
        exps = jnp.where(allowed[None, None], jnp.exp(scores - new_max[..., None]), 0.0)
        factor = jnp.exp(running_max - new_max)
        new_sum = running_sum * factor + jnp.sum(exps, axis=-1)
        new_acc = running_acc * factor[..., None] + jnp.einsum(
            "kgtn,nkd->kgtd",
            exps.astype(jnp.bfloat16),
            value_block,
            preferred_element_type=jnp.float32,
        )
        inner = (new_max, new_sum, new_acc)
        return (inner, None)

    state, _ = lax.scan(advance, state, (key_blocks, value_blocks, key_positions, key_segments))
    final_max, final_sum, final_acc = state
    mixed = final_acc / final_sum[..., None]
    return (
        jnp.transpose(mixed, (2, 0, 1, 3))
        .reshape(tok_rows, heads_here * head_size)
        .astype(jnp.bfloat16)
    )


BLOCK = 256
NEG = -1e30


def fused_kernel(
    tokens, gain, w_query, w_key, w_value, table, bounds, kpos, out,
    wall, normed, acc, qrot, kv, lsem, cs, cr, xs, xr, ys, yr, fs, fr, hs, hr, kvs, kvr,
):
    g = lax.axis_index("groups")
    t = lax.axis_index("ctx")
    m = lax.axis_index("mp")
    x_index = t // 2
    core = t % 2
    t_core = x_index * 2 + (1 - core)
    t_x = (1 - x_index) * 2 + core
    t_diag = (1 - x_index) * 2 + (1 - core)
    shard_rows = w_query.shape[0]
    half = shard_rows // 2
    rows = tokens.shape[0]
    kv_cols = w_key.shape[1]
    blocks = wall.shape[0]
    kv_heads = kv_cols // HEAD_SIZE
    group_width = w_query.shape[1] // kv_cols
    kv_blocks = 2 * kv_cols // BLOCK
    core_dev = (g, t_core, m)
    x_dev = (g, t_x, m)
    y_dev = (1 - g, t, m)

    def remote(src, dst, send, recv, dev):
        return pltpu.make_async_remote_copy(
            src_ref=src, dst_ref=dst, send_sem=send, recv_sem=recv,
            device_id=dev, device_id_type=pl.DeviceIdType.MESH,
        )

    def piece(b, shard, h):
        return wall.at[b, shard, pl.ds(pl.multiple_of(h * half, half), half), :]

    def core_send(b):
        return remote(wall.at[b, t], wall.at[b, t], cs.at[b], cr.at[b], core_dev)

    def x_send(b):
        return remote(piece(b, t, g), piece(b, t, g), xs.at[b], xr.at[b], x_dev)

    def y_send(b):
        return remote(piece(b, t_x, g), piece(b, t_x, g), ys.at[b], yr.at[b], y_dev)

    def core_x(b):
        return remote(piece(b, t_x, g), piece(b, t_x, g), fs.at[b], fr.at[b], core_dev)

    def core_y(b):
        return remote(piece(b, t_x, 1 - g), piece(b, t_x, 1 - g), hs.at[b], hr.at[b], core_dev)

    def kv_copy(index, shard, dev):
        view = kv.at[pl.ds(pl.multiple_of(shard * rows, rows), rows), :]
        return remote(view, view, kvs.at[index], kvr.at[index], dev)

    token_copy = pltpu.make_async_copy(tokens, normed, lsem.at[blocks])
    local_copies = []
    for b in range(blocks):
        if b < kv_blocks // 2:
            source = w_key.at[:, pl.ds(b * BLOCK, BLOCK)]
        elif b < kv_blocks:
            source = w_value.at[:, pl.ds((b - kv_blocks // 2) * BLOCK, BLOCK)]
        else:
            source = w_query.at[:, pl.ds((b - kv_blocks) * BLOCK, BLOCK)]
        local_copies.append(pltpu.make_async_copy(source, wall.at[b, t], lsem.at[b]))
    local_copies[0].start()
    token_copy.start()
    for copy in local_copies[1:]:
        copy.start()

    barrier = pltpu.get_barrier_semaphore()
    for dev in (core_dev, x_dev, y_dev):
        pl.semaphore_signal(barrier, inc=1, device_id=dev, device_id_type=pl.DeviceIdType.MESH)
    pl.semaphore_wait(barrier, 3)

    for b in range(blocks):
        local_copies[b].wait()
        if b < AHEAD:
            x_send(b).start()
            core_send(b).start()
    token_copy.wait()

    gain_row = gain[...].astype(jnp.float32)

    def norm_rows(i, carry):
        at = pl.ds(pl.multiple_of(i * 16, 16), 16)
        floats = normed[at, :].astype(jnp.float32)
        inverse = lax.rsqrt(jnp.mean(floats * floats, axis=-1, keepdims=True) + 1e-05)
        normed[at, :] = (floats * inverse * gain_row).astype(jnp.bfloat16)
        return carry

    lax.fori_loop(0, rows // 16, norm_rows, 0)

    def product(b, shard, h):
        columns = pl.ds(pl.multiple_of(shard * shard_rows + h * half, half), half)
        return jnp.dot(
            normed[:, columns],
            wall[b, shard, pl.ds(pl.multiple_of(h * half, half), half), :],
            preferred_element_type=jnp.float32,
        )

    def turned(head):
        first = acc[:, head * HEAD_SIZE : (head + 1) * HEAD_SIZE]
        swapped = pltpu.roll(first, HEAD_SIZE // 2, 1)
        return (first * table[0] + swapped * table[1]).astype(jnp.bfloat16)

    factor = (HEAD_SIZE ** (-0.5)) * math.log2(math.e)
    tile = 128

    def attend(b):
        heads = BLOCK // HEAD_SIZE
        first_head = (b - kv_blocks) * heads

        def one(step, carry):
            h = step % heads
            r = step // heads
            at = pl.ds(pl.multiple_of(r * tile, tile), tile)
            kv_head = (first_head + h) // group_width
            kcol = pl.ds(pl.multiple_of(kv_head * HEAD_SIZE, HEAD_SIZE), HEAD_SIZE)
            vcol = pl.ds(pl.multiple_of(kv_cols + kv_head * HEAD_SIZE, HEAD_SIZE), HEAD_SIZE)
            scores = lax.dot_general(
                qrot[at, pl.ds(pl.multiple_of(h * HEAD_SIZE, HEAD_SIZE), HEAD_SIZE)],
                kv[:, kcol],
                (((1,), (1,)), ((), ())),
                preferred_element_type=jnp.float32,
            )
            keys = kpos[...]
            allowed = (keys <= bounds[0, at, :]) & (keys >= bounds[1, at, :])
            scores = jnp.where(allowed, scores, NEG)
            peak = jnp.max(scores, axis=-1, keepdims=True)
            exps = jnp.exp2((scores - peak) * factor)
            total = jnp.sum(exps, axis=-1, keepdims=True)
            mixed = jnp.dot(exps.astype(jnp.bfloat16), kv[:, vcol], preferred_element_type=jnp.float32)
            ocol = pl.ds(pl.multiple_of((first_head + h) * HEAD_SIZE, HEAD_SIZE), HEAD_SIZE)
            out[at, ocol] = (mixed / total).astype(jnp.bfloat16)
            return carry

        lax.fori_loop(0, heads * (rows // tile), one, 0)

    x_send(0).wait_recv()
    y_send(0).start()
    core_x(0).start()
    mine = pl.ds(pl.multiple_of(t * rows, rows), rows)

    def block(b, carry):
        core_send(b).wait_recv()

        def own(i, c):
            acc[...] += product(b, x_index * 2 + (core + i // 2) % 2, i % 2)
            return c

        acc[...] = jnp.zeros_like(acc)
        lax.fori_loop(0, 4, own, 0)
        core_x(b).wait_recv()

        def crossed(i, c):
            acc[...] += product(b, (1 - x_index) * 2 + (core + i) % 2, g)
            return c

        lax.fori_loop(0, 2, crossed, 0)

        @pl.when(b + 1 < blocks)
        def _():
            x_send(b + 1).wait_recv()
            y_send(b + 1).start()
            core_x(b + 1).start()

        @pl.when(b + AHEAD < blocks)
        def _():
            x_send(b + AHEAD).start()
            core_send(b + AHEAD).start()

        @pl.when(b == kv_blocks)
        def _():
            kv_copy(1, t, x_dev).wait_recv()
            kv_copy(2, t_x, core_dev).start()

        y_send(b).wait_recv()
        core_y(b).start()

        acc[...] += product(b, t_x, 1 - g)
        core_y(b).wait_recv()
        acc[...] += product(b, t_diag, 1 - g)

        @pl.when(b == 0)
        def _():
            for head in range(kv_heads):
                kv[mine, pl.ds(head * HEAD_SIZE, HEAD_SIZE)] = turned(head)

        @pl.when(b == 1)
        def _():
            kv[mine, pl.ds(kv_cols, kv_cols)] = acc[...].astype(jnp.bfloat16)
            kv_copy(1, t, x_dev).start()
            kv_copy(0, t, core_dev).start()

        @pl.when(b == kv_blocks)
        def _():
            kv_copy(0, t, core_dev).wait_recv()
            kv_copy(2, t_x, core_dev).wait_recv()

        @pl.when(b >= kv_blocks)
        def _():
            for head in range(BLOCK // HEAD_SIZE):
                qrot[:, pl.ds(head * HEAD_SIZE, HEAD_SIZE)] = turned(head)
            attend(b)

        return carry

    lax.fori_loop(0, blocks, block, 0)

    def drain(b, carry):
        core_send(b).wait_send()
        x_send(b).wait_send()
        y_send(b).wait_send()
        core_x(b).wait_send()
        core_y(b).wait_send()
        return carry

    lax.fori_loop(0, blocks, drain, 0)
    kv_copy(0, t, core_dev).wait_send()
    kv_copy(1, t, x_dev).wait_send()
    kv_copy(2, t_x, core_dev).wait_send()


AHEAD = 3


def local_fused(tokens, norm_gain, w_query, w_key, value_weight, slab_order, segment_ids):
    rows, width = tokens.shape
    slabs = slab_order.shape[0]
    places = jnp.arange(rows, dtype=jnp.int32)
    my_position = slab_order[lax.axis_index("ctx")] * rows + places
    key_positions = (slab_order[:, None] * rows + places[None, :]).reshape(1, slabs * rows)
    starts = jnp.sum(
        (segment_ids[None, :] < jnp.arange(1, 4, dtype=jnp.int32)[:, None]).astype(jnp.int32), axis=1
    )
    lowest = jnp.max(
        jnp.where(my_position[:, None] >= starts[None, :], starts[None, :], 0), axis=1
    )
    bounds = jnp.stack([my_position, lowest])[:, :, None]
    half = HEAD_SIZE // 2
    freqs = jnp.exp(jnp.arange(half, dtype=jnp.float32) * (-2.0 * math.log(500000.0) / HEAD_SIZE))
    angles = my_position.astype(jnp.float32)[:, None] * freqs[None, :]
    cosine = jnp.cos(angles)
    sine = jnp.sin(angles)
    table = jnp.stack(
        [jnp.concatenate([cosine, cosine], axis=1), jnp.concatenate([-sine, sine], axis=1)]
    )
    shard_rows, query_cols = w_query.shape
    kv_cols = w_key.shape[1]
    blocks = (query_cols + 2 * kv_cols) // BLOCK
    whole = pl.BlockSpec(memory_space=pltpu.VMEM)
    hbm = pl.BlockSpec(memory_space=pl.ANY)
    sems = pltpu.SemaphoreType.DMA((blocks,))
    columns = query_cols + 2 * kv_cols
    return pl.pallas_call(
        fused_kernel,
        out_shape=jax.ShapeDtypeStruct((rows, query_cols), jnp.bfloat16),
        in_specs=[hbm, whole, hbm, hbm, hbm, whole, whole, whole],
        out_specs=whole,
        scratch_shapes=[
            pltpu.VMEM((blocks, 4, shard_rows, BLOCK), jnp.bfloat16),
            pltpu.VMEM((rows, width), jnp.bfloat16),
            pltpu.VMEM((rows, BLOCK), jnp.float32),
            pltpu.VMEM((rows, BLOCK), jnp.bfloat16),
            pltpu.VMEM((slabs * rows, 2 * kv_cols), jnp.bfloat16),
            pltpu.SemaphoreType.DMA((blocks + 1,)),
            sems, sems, sems, sems, sems, sems, sems, sems, sems, sems,
            pltpu.SemaphoreType.DMA((3,)),
            pltpu.SemaphoreType.DMA((3,)),
        ],
        compiler_params=pltpu.CompilerParams(
            collective_id=0, has_side_effects=True, vmem_limit_bytes=58 << 20
        ),
        cost_estimate=pl.CostEstimate(
            flops=2 * rows * width * columns, bytes_accessed=40 << 20, transcendentals=rows * slabs * rows * 8
        ),
    )(
        tokens, norm_gain.reshape(1, width), w_query, w_key, value_weight,
        table, bounds, key_positions,
    )


def solution(mesh):
    small = mesh.shape["ctx"] == 4 and mesh.shape["groups"] == 2 and mesh.shape["mp"] == 4
    local = local_fused if small else local_plain
    return jax.shard_map(
        local,
        mesh=mesh,
        in_specs=(
            P(("groups", "ctx"), None),
            P(),
            P("ctx", "mp"),
            P("ctx", "mp"),
            P("ctx", "mp"),
            P("groups"),
            P("groups"),
        ),
        out_specs=P(("groups", "ctx"), "mp"),
        check_vma=False,
    )
```
